256 devices in a mesh: row: 16 (over z_lo, x, core), col: 16 (over y, z_hi).
Axes of the slice: x: 4, y: 4, z: 8 (z_hi: 4, z_lo: 2; z = z_hi * 2 + z_lo), core: 2. Of those that a mesh axis runs over, the one named last changes fastest.
Arguments:
- left_factor: bfloat16 [128, 32, 2048], P('col', None, 'row'), may hold values from -6 to 6
- right_factor: bfloat16 [128, 32, 2048], P('row', None, 'col'), may hold values from -6 to 6
- pair_grad: bfloat16 [2048, 128, 2048], P('row', None, 'col'), may hold values from -6 to 6
- projection: bfloat16 [1024, 128], replicated, may hold values from -0.1875 to 0.1875
Outputs:
- left_grad: float32 [128, 32, 2048], P('col', None, 'row')
- right_grad: float32 [128, 32, 2048], P('row', None, 'col')
The draws below stay inside these ranges and needn't reach their ends.
All inputs are finite; a program needn't handle non-finite values.
Results may differ from the reference program's by a relative error of at most 0.0029.
Values may be sent and summed in bfloat16 or wider, within the bound.
No kernel may reach another device: no remote copies, remote signals or barrier semaphores. Data moves between devices by JAX's collectives and lax.ppermute only.
A program may use at most 256 MiB of HBM per device.

```python
import jax
import jax.numpy as jnp
from jax import lax

C = 32
CZ = 128
NRES = 2048
SEQS = 128


def level_of(key, extent, split, least, high):
    def one(position, shards_of):
        steps = jax.random.uniform(jax.random.fold_in(jax.random.fold_in(key, 6), position), (shards_of,), jnp.float32, least / len(split), high / len(split))
        return jnp.repeat(jnp.exp(steps), extent[position] // shards_of).reshape((-1,) + (1,) * (len(extent) - position - 1))

    level = one(*split[0])
    for cut in split[1:]:
        level = level * one(*cut)
    return level


def normal_values(stream_key, extent, deviation, bound, shards=(), dtype=jnp.bfloat16):
    loudness = level_of(stream_key, extent, shards, -0.22, 0.18) if shards else 1.0
    drawn = jax.random.normal(stream_key, extent, jnp.float32) * deviation * loudness
    return jnp.minimum(jnp.maximum(drawn, -bound), bound).astype(dtype)


def setup_inputs(seed: int = 0) -> dict:
    key_of = jax.random.split(jax.random.key(seed), 5)
    left_factor = normal_values(key_of[0], (SEQS, C, NRES), 1.0, 6.0, ((0, 16), (2, 16)))
    right_factor = normal_values(key_of[1], (SEQS, C, NRES), 1.0, 6.0, ((0, 16), (2, 16)))
    pair_grad = normal_values(key_of[2], (NRES, CZ, NRES), 1.0, 6.0, ((0, 16), (2, 16)))
    projection = normal_values(key_of[3], (C * C, CZ), (C * C) ** -0.5, 0.1875)
    return {"left_factor": left_factor, "right_factor": right_factor, "pair_grad": pair_grad, "projection": projection}


def reference(left_factor, right_factor, pair_grad, projection):
    total = pair_grad.shape[0]
    height = 32
    counted = total // height
    inverse = 1.0 / SEQS
    left_wide = left_factor.astype(jnp.float32)
    right_wide = right_factor.astype(jnp.float32)

    def advance(right_sum, offset):
        slab = lax.dynamic_slice_in_dim(pair_grad, offset, height, 0)
        slab = jnp.moveaxis(slab, 1, 2)
        expanded = jnp.dot(slab.reshape(height * total, CZ), projection.T, preferred_element_type=jnp.float32)
        expanded = expanded.astype(jnp.bfloat16).astype(jnp.float32).reshape(height, total, C, C)
        left_piece = jnp.einsum("ijce,sej->sci", expanded, right_wide) * inverse
        left_slab = lax.dynamic_slice_in_dim(left_wide, offset, height, 2)
        right_sum = right_sum + jnp.einsum("ijce,sci->sej", expanded, left_slab)
        return right_sum, left_piece

    offsets = (jnp.arange(counted) * height).astype(jnp.int32)
    right_sum, left_pieces = lax.scan(advance, jnp.zeros((SEQS, C, total), jnp.float32), offsets)
    left_grad = jnp.moveaxis(left_pieces, 0, 2).reshape(SEQS, C, total)
    right_grad = right_sum * inverse
    return left_grad, right_grad
```

```python
import jax
import jax.numpy as jnp
from jax import lax
from jax.experimental import pallas as pl
from jax.experimental.pallas import tpu as pltpu
from jax.sharding import Mesh
from jax.sharding import PartitionSpec as P

ROW = ("z_lo", "x", "core")
COL = ("y", "z_hi")
VMEM = 48 << 20


def expand(pair_grad, weights, channels, group):
    rows, width, cols = pair_grad.shape
    wide = weights.shape[0]
    entries = wide // channels
    step = 8

    def body(weight_ref, grad_ref, out_ref):
        for i in range(0, group, 2):
            pair = jnp.concatenate([grad_ref[i], grad_ref[i + 1]], axis=1)
            for first in range(0, entries, step):
                piece = weight_ref[first * channels : (first + step) * channels, :]
                value = jnp.dot(piece, pair, preferred_element_type=jnp.float32).astype(jnp.bfloat16)
                for k in range(step):
                    for half in range(2):
                        top = (i + half) * channels
                        side = (first + k) * cols
                        out_ref[top : top + channels, side : side + cols] = value[
                            k * channels : (k + 1) * channels, half * cols : (half + 1) * cols
                        ]

    return pl.pallas_call(
        body,
        grid=(rows // group,),
        in_specs=[
            pl.BlockSpec((wide, width), lambda i: (0, 0)),
            pl.BlockSpec((group, width, cols), lambda i: (i, 0, 0)),
        ],
        out_specs=pl.BlockSpec((group * channels, entries * cols), lambda i: (i, 0)),
        out_shape=jax.ShapeDtypeStruct((rows * channels, entries * cols), jnp.bfloat16),
        compiler_params=pltpu.CompilerParams(vmem_limit_bytes=VMEM),
        name="expand",
    )(weights, pair_grad)


def left_partial(right_flat, expanded, inverse, block):
    sequences, depth = right_flat.shape
    total = expanded.shape[0]

    def body(right_ref, expanded_ref, out_ref):
        value = lax.dot_general(
            right_ref[...], expanded_ref[...], (((1,), (1,)), ((), ())), preferred_element_type=jnp.float32
        )
        out_ref[...] = (value * inverse).astype(jnp.bfloat16)

    return pl.pallas_call(
        body,
        grid=(total // block,),
        in_specs=[
            pl.BlockSpec((sequences, depth), lambda i: (0, 0)),
            pl.BlockSpec((block, depth), lambda i: (i, 0)),
        ],
        out_specs=pl.BlockSpec((sequences, block), lambda i: (0, i)),
        out_shape=jax.ShapeDtypeStruct((sequences, total), jnp.bfloat16),
        compiler_params=pltpu.CompilerParams(vmem_limit_bytes=VMEM),
        name="left_partial",
    )(right_flat, expanded)


def right_partial(left_flat, expanded, inverse, block):
    sequences, depth = left_flat.shape
    total = expanded.shape[1]

    def body(left_ref, expanded_ref, out_ref):
        value = jnp.dot(left_ref[...], expanded_ref[...], preferred_element_type=jnp.float32)
        out_ref[...] = (value * inverse).astype(jnp.bfloat16)

    return pl.pallas_call(
        body,
        grid=(total // block,),
        in_specs=[
            pl.BlockSpec((sequences, depth), lambda i: (0, 0)),
            pl.BlockSpec((depth, block), lambda i: (0, i)),
        ],
        out_specs=pl.BlockSpec((sequences, block), lambda i: (0, i)),
        out_shape=jax.ShapeDtypeStruct((sequences, total), jnp.bfloat16),
        compiler_params=pltpu.CompilerParams(vmem_limit_bytes=VMEM),
        name="right_partial",
    )(left_flat, expanded)


def gathered(shard, axes):
    count = lax.axis_size(axes)
    copies = jnp.broadcast_to(shard[None], (count,) + shard.shape)
    blocks = lax.all_to_all(copies, axes, 0, 0, tiled=True)
    return blocks.reshape((count * shard.shape[0],) + shard.shape[1:])


def sent_and_summed(partial, axes):
    count = lax.axis_size(axes)
    blocks = partial.reshape((count, partial.shape[0] // count) + partial.shape[1:])
    blocks = lax.all_to_all(blocks, axes, 0, 0, tiled=True)
    return jnp.sum(blocks.astype(jnp.float32), axis=0)


def on_device(left_factor, right_factor, pair_grad, projection):
    shared, channels, rows = left_factor.shape
    held, entries, cols = right_factor.shape
    left_flat = jnp.transpose(left_factor, (0, 2, 1)).reshape(shared, rows * channels)
    right_flat = right_factor.reshape(held, entries * cols)
    right_whole = gathered(right_flat, ROW)
    left_whole = gathered(left_flat, COL)
    inverse = 1.0 / left_whole.shape[0]
    weights = jnp.swapaxes(projection.reshape(channels, entries, -1), 0, 1).reshape(projection.shape)
    expanded = expand(pair_grad, weights, channels, 16)
    left_sum = left_partial(right_whole, expanded, inverse, 512)
    left_grad = sent_and_summed(left_sum, COL)
    right_sum = right_partial(left_whole, expanded, inverse, 1024)
    right_grad = sent_and_summed(right_sum, ROW)
    left_grad = jnp.swapaxes(left_grad.reshape(shared, rows, channels), 1, 2)
    return (left_grad, right_grad.reshape(held, entries, cols))


def solution(mesh):
    names = ("z_lo", "x", "core", "y", "z_hi")
    torus = Mesh(mesh.devices.reshape(2, 4, 2, 4, 4), names)
    return jax.shard_map(
        on_device,
        mesh=torus,
        in_specs=(P(COL, None, ROW), P(ROW, None, COL), P(ROW, None, COL), P()),
        out_specs=(P(COL, None, ROW), P(ROW, None, COL)),
        check_vma=False,
    )
```

```python
import jax
import jax.numpy as jnp
from jax import lax
from jax.experimental import pallas as pl
from jax.experimental.pallas import tpu as pltpu
from jax.sharding import Mesh
from jax.sharding import PartitionSpec as P

ROW = ("z_lo", "x", "core")
COL = ("y", "z_hi")
VMEM = 12 << 20
PIECES = 4
WHOLE = pl.BlockSpec(memory_space=pltpu.VMEM)
TABLE = pl.BlockSpec(memory_space=pltpu.SMEM)


def params():
    return pltpu.CompilerParams(vmem_limit_bytes=VMEM)


def expand(pair_grad, weights, channels, number):
    rows, width, cols = pair_grad.shape
    wide = weights.shape[0]
    entries = wide // channels
    held = rows // PIECES
    step = 8

    def body(weight_ref, grad_ref, out_ref):
        def two(t, carry):
            i = number * held + t * 2
            pair = jnp.concatenate([grad_ref[i], grad_ref[i + 1]], axis=1)
            base = pl.multiple_of(t * (2 * channels), 2 * channels)
            for first in range(0, entries, step):
                piece = weight_ref[first * channels : (first + step) * channels, :]
                value = jnp.dot(piece, pair, preferred_element_type=jnp.float32).astype(jnp.bfloat16)
                for k in range(step):
                    block = value[k * channels : (k + 1) * channels]
                    stacked = jnp.concatenate([block[:, :cols], block[:, cols:]], axis=0)
                    side = (first + k) * cols
                    out_ref[pl.ds(base, 2 * channels), side : side + cols] = stacked
            return carry

        lax.fori_loop(0, held // 2, two, 0, unroll=2)

    return pl.pallas_call(
        body,
        in_specs=[WHOLE, WHOLE],
        out_specs=WHOLE,
        out_shape=pltpu.VMEM((held * channels, entries * cols), jnp.bfloat16),
        compiler_params=params(),
        cost_estimate=pl.CostEstimate(flops=4 * held * wide * width * cols, transcendentals=0, bytes_accessed=1 << 20),
        name="expand",
    )(weights, pair_grad)


def place(scratch, table_ref, sources, size):
    at = 0
    for source in sources:
        for top in range(0, source.shape[0], size):
            scratch[table_ref[at]] = source[top : top + size, :]
            at += 1


def left_partial(table, sources, expanded, size, inverse):
    count = table.shape[0]
    sequences = count * size
    depth = expanded[0].shape[1]
    total = sum(e.shape[0] for e in expanded)
    part = sequences // 4
    block = 512

    def body(table_ref, *refs):
        source_refs = refs[: len(sources)]
        expanded_refs = refs[len(sources) : len(sources) + len(expanded)]
        own_ref, *other_refs = refs[len(sources) + len(expanded) : -2]
        placed, turned = refs[-2:]
        place(placed, table_ref, source_refs, size)
        turned[...] = placed[...].reshape(sequences, depth).T
        at = 0
        for expanded_ref in expanded_refs:
            for top in range(0, expanded_ref.shape[0], block):
                value = jnp.dot(
                    expanded_ref[top : top + block, :], turned[...], preferred_element_type=jnp.float32
                )
                value = value.T * inverse
                own_ref[:, at : at + block] = value[:part]
                for k, other_ref in enumerate(other_refs):
                    lower = (k + 1) * part
                    other_ref[:, at : at + block] = value[lower : lower + part].astype(jnp.bfloat16)
                at += block

    other = jax.ShapeDtypeStruct((part, total), jnp.bfloat16)
    return pl.pallas_call(
        body,
        in_specs=[TABLE] + [WHOLE] * (len(sources) + len(expanded)),
        out_specs=[WHOLE] * 4,
        out_shape=[jax.ShapeDtypeStruct((part, total), jnp.float32), other, other, other],
        scratch_shapes=[pltpu.VMEM((count, size, depth), jnp.bfloat16), pltpu.VMEM((depth, sequences), jnp.bfloat16)],
        compiler_params=params(),
        cost_estimate=pl.CostEstimate(flops=4 * sequences * depth * total, transcendentals=0, bytes_accessed=1 << 20),
        name="left_partial",
    )(table, *sources, *expanded)


def right_partial(table, sources, expanded, size, inverse):
    count = table.shape[0]
    sequences = count * size
    depth = sum(e.shape[0] for e in expanded)
    total = expanded[0].shape[1]
    part = sequences // 2
    block = 512

    def body(table_ref, *refs):
        source_refs = refs[: len(sources)]
        expanded_refs = refs[len(sources) : len(sources) + len(expanded)]
        own_ref, other_ref, blocked, placed = refs[len(sources) + len(expanded) :]
        place(blocked, table_ref, source_refs, size)
        placed[...] = blocked[...].reshape(sequences, depth)
        for side in range(0, total, block):
            value = 0.0
            at = 0
            for expanded_ref in expanded_refs:
                high = expanded_ref.shape[0]
                value = value + jnp.dot(
                    placed[:, at : at + high],
                    expanded_ref[:, side : side + block],
                    preferred_element_type=jnp.float32,
                )
                at += high
            value = value * inverse
            own_ref[:, side : side + block] = value[:part]
            other_ref[:, side : side + block] = value[part:]

    half = jax.ShapeDtypeStruct((part, total), jnp.float32)
    return pl.pallas_call(
        body,
        in_specs=[TABLE] + [WHOLE] * (len(sources) + len(expanded)),
        out_specs=[WHOLE] * 2,
        out_shape=[half, half],
        scratch_shapes=[pltpu.VMEM((count, size, depth), jnp.bfloat16), pltpu.VMEM((sequences, depth), jnp.bfloat16)],
        compiler_params=params(),
        cost_estimate=pl.CostEstimate(flops=2 * sequences * depth * total, transcendentals=0, bytes_accessed=1 << 20),
        name="right_partial",
    )(table, *sources, *expanded)


def moved(value, axis, distance):
    size = lax.axis_size(axis)
    return lax.ppermute(value, axis, [(k, (k + distance) % size) for k in range(size)])


def swapped(value, axis, bit):
    return lax.ppermute(value, axis, [(k, k ^ bit) for k in range(lax.axis_size(axis))])


def orders(blocks):
    z_lo, x, core, y, z_hi = (lax.axis_index(name) for name in ROW + COL)
    at = lax.iota(jnp.int32, blocks)
    block = (z_lo ^ (at // 4 % 2)) * 8 + (x - at) % 4 * 2 + (core ^ (at // 8))
    left_table = (block // 4 - y) % 4 * 4 + (block - z_hi) % 4
    block = (y - at // 4) % 4 * 4 + (z_hi ^ (at % 4))
    right_table = (block - core) % 2 * 8 + (block // 8 - z_lo) % 2 * 4 + (block // 2 - x) % 4
    return left_table, right_table


def on_device(left_factor, right_factor, pair_grad, projection):
    shared, channels, rows = left_factor.shape
    held, entries, cols = right_factor.shape
    left_flat = jnp.transpose(left_factor, (0, 2, 1)).reshape(shared, rows * channels)
    right_flat = right_factor.reshape(held, entries * cols)
    weights = jnp.swapaxes(projection.reshape(channels, entries, -1), 0, 1).reshape(projection.shape)

    blocks = 4 * 4
    inverse = 1.0 / (blocks * shared)
    left_table, right_table = orders(blocks)
    left_table, right_table, pair_grad = lax.optimization_barrier((left_table, right_table, pair_grad))

    along_x = jnp.concatenate([right_flat] + [moved(right_flat, "x", d) for d in (1, 2, 3)], axis=0)
    near_left = jnp.concatenate([left_flat, swapped(left_flat, "z_hi", 1)], axis=0)
    near_left = jnp.concatenate([near_left, swapped(near_left, "z_hi", 2)], axis=0)
    along_z = jnp.concatenate([along_x, swapped(along_x, "z_lo", 1)], axis=0)
    along_core = swapped(along_z, "core", 1)

    expanded = [expand(pair_grad, weights, channels, number) for number in range(PIECES)]
    own, *others = left_partial(left_table, [along_z, along_core], expanded, held, inverse)

    far_left = [near_left] + [moved(near_left, "y", d) for d in (1, 2, 3)]
    right_table, others = lax.optimization_barrier((right_table, others))
    right_own, right_other = right_partial(right_table, far_left, expanded, shared, inverse)

    left_sum = own
    for d, other in enumerate(others):
        left_sum = left_sum + moved(other, "y", d + 1).astype(jnp.float32)
    left_grad = left_sum[:shared]
    for d in (1, 2, 3):
        piece = left_sum[d * shared : (d + 1) * shared].astype(jnp.bfloat16)
        left_grad = left_grad + moved(piece, "z_hi", d).astype(jnp.float32)
    left_grad = jnp.swapaxes(left_grad.reshape(shared, rows, channels), 1, 2)

    right_sum = right_own + swapped(right_other, "core", 1)
    middle = 4 * held
    right_sum = right_sum[:middle] + swapped(right_sum[middle:].astype(jnp.bfloat16), "z_lo", 1).astype(jnp.float32)
    right_grad = right_sum[:held]
    for d in (1, 2, 3):
        piece = right_sum[d * held : (d + 1) * held].astype(jnp.bfloat16)
        right_grad = right_grad + moved(piece, "x", d).astype(jnp.float32)
    return (left_grad, right_grad.reshape(held, entries, cols))


def solution(mesh):
    names = ("z_lo", "x", "core", "y", "z_hi")
    torus = Mesh(mesh.devices.reshape(2, 4, 2, 4, 4), names)
    return jax.shard_map(
        on_device,
        mesh=torus,
        in_specs=(P(COL, None, ROW), P(ROW, None, COL), P(ROW, None, COL), P()),
        out_specs=(P(COL, None, ROW), P(ROW, None, COL)),
        check_vma=False,
    )
```

```python
import jax
import jax.numpy as jnp
from jax import lax
from jax.experimental import pallas as pl
from jax.experimental.pallas import tpu as pltpu
from jax.sharding import Mesh
from jax.sharding import PartitionSpec as P

ROW = ("z_lo", "x", "core")
COL = ("y", "z_hi")
VMEM = 12 << 20
PIECES = 4
WHOLE = pl.BlockSpec(memory_space=pltpu.VMEM)
TABLE = pl.BlockSpec(memory_space=pltpu.SMEM)


def params():
    return pltpu.CompilerParams(vmem_limit_bytes=VMEM)


def expand(pair_grad, weights, channels, number, after=()):
    rows, width, cols = pair_grad.shape
    wide = weights.shape[0]
    entries = wide // channels
    held = rows // PIECES
    step = 2
    chunk = 8
    first = number == 0

    def body(weight_ref, grad_ref, *rest):
        out_ref, token_ref, *rest = rest[len(after) :]
        copies = []
        if first:
            source_ref = grad_ref
            grad_ref, sems = rest
            for k in range(rows // chunk):
                part = pl.ds(k * chunk, chunk)
                copies.append(pltpu.make_async_copy(source_ref.at[part], grad_ref.at[part], sems.at[k]))
                copies[k].start()
        for t in range(held // 2):
            if first and t * 2 % chunk == 0:
                copies[t * 2 // chunk].wait()
            i = number * held + t * 2
            pair = jnp.concatenate([grad_ref[i], grad_ref[i + 1]], axis=1)
            base = t * 2 * channels
            for entry in range(0, entries, step):
                piece = weight_ref[entry * channels : (entry + step) * channels, :]
                value = jnp.dot(piece, pair, preferred_element_type=jnp.float32).astype(jnp.bfloat16)
                for k in range(step):
                    block = value[k * channels : (k + 1) * channels]
                    stacked = jnp.concatenate([block[:, :cols], block[:, cols:]], axis=0)
                    side = (entry + k) * cols
                    out_ref[base : base + 2 * channels, side : side + cols] = stacked
        for copy in copies[held // chunk :]:
            copy.wait()
        token_ref[...] = out_ref[:16, :128]

    moved_shape = pltpu.VMEM(pair_grad.shape, pair_grad.dtype)
    return pl.pallas_call(
        body,
        in_specs=[WHOLE, pl.BlockSpec(memory_space=pltpu.HBM) if first else WHOLE] + [WHOLE] * len(after),
        out_specs=[WHOLE] * (3 if first else 2),
        out_shape=[
            pltpu.VMEM((held * channels, entries * cols), jnp.bfloat16),
            jax.ShapeDtypeStruct((16, 128), jnp.bfloat16),
        ]
        + ([moved_shape] if first else []),
        scratch_shapes=[pltpu.SemaphoreType.DMA((rows // chunk,))] if first else [],
        compiler_params=params(),
        cost_estimate=pl.CostEstimate(flops=4 * held * wide * width * cols, transcendentals=0, bytes_accessed=1 << 20),
        name="expand",
    )(weights, pair_grad, *after)


def join(groups, after):
    parts = [part for group in groups for part in group]

    def body(*refs):
        source_refs = refs[: len(parts)]
        out_refs = refs[len(parts) + len(after) : -1]
        at = 0
        for group, out_ref in zip(groups, out_refs):
            top = 0
            for part in group:
                out_ref[top : top + part.shape[0], :] = source_refs[at][...]
                top += part.shape[0]
                at += 1
        refs[-1][...] = refs[len(parts)][...]

    shapes = [(sum(part.shape[0] for part in group), group[0].shape[1]) for group in groups] + [after[0].shape]
    return pl.pallas_call(
        body,
        in_specs=[WHOLE] * (len(parts) + len(after)),
        out_specs=[WHOLE] * len(shapes),
        out_shape=[jax.ShapeDtypeStruct(shape, jnp.bfloat16) for shape in shapes],
        compiler_params=params(),
        cost_estimate=pl.CostEstimate(flops=0, transcendentals=0, bytes_accessed=1 << 20),
        name="join",
    )(*parts, *after)


def place(scratch, table_ref, sources, size):
    at = 0
    for source in sources:
        for top in range(0, source.shape[0], size):
            scratch[table_ref[at]] = source[top : top + size, :]
            at += 1


def left_partial(table, sources, expanded, size, inverse):
    count = table.shape[0]
    sequences = count * size
    depth = expanded[0].shape[1]
    total = sum(e.shape[0] for e in expanded)
    part = sequences // 4
    block = 512

    def body(table_ref, *refs):
        source_refs = refs[: len(sources)]
        expanded_refs = refs[len(sources) : len(sources) + len(expanded)]
        token_ref, own_ref, *other_refs = refs[len(sources) + len(expanded) : -2]
        placed, turned = refs[-2:]
        place(placed, table_ref, source_refs, size)
        turned[...] = placed[...].reshape(sequences, depth).T
        at = 0
        for expanded_ref in expanded_refs:
            for top in range(0, expanded_ref.shape[0], block):
                value = jnp.dot(
                    expanded_ref[top : top + block, :], turned[...], preferred_element_type=jnp.float32
                )
                value = value.T * inverse
                own_ref[:, at : at + block] = value[:part]
                for k, other_ref in enumerate(other_refs):
                    lower = (k + 1) * part
                    other_ref[:, at : at + block] = value[lower : lower + part].astype(jnp.bfloat16)
                at += block
        token_ref[...] = other_refs[0][:16, :128]

    other = jax.ShapeDtypeStruct((part, total), jnp.bfloat16)
    return pl.pallas_call(
        body,
        in_specs=[TABLE] + [WHOLE] * (len(sources) + len(expanded)),
        out_specs=[WHOLE] * 5,
        out_shape=[
            jax.ShapeDtypeStruct((16, 128), jnp.bfloat16),
            jax.ShapeDtypeStruct((part, total), jnp.float32),
            other,
            other,
            other,
        ],
        scratch_shapes=[pltpu.VMEM((count, size, depth), jnp.bfloat16), pltpu.VMEM((depth, sequences), jnp.bfloat16)],
        compiler_params=params(),
        cost_estimate=pl.CostEstimate(flops=4 * sequences * depth * total, transcendentals=0, bytes_accessed=1 << 20),
        name="left_partial",
    )(table, *sources, *expanded)


def right_partial(table, sources, expanded, size, inverse, after):
    count = table.shape[0]
    sequences = count * size
    depth = sum(e.shape[0] for e in expanded)
    total = expanded[0].shape[1]
    part = sequences // 2
    block = 512

    def body(table_ref, *refs):
        source_refs = refs[: len(sources)]
        expanded_refs = refs[len(sources) : len(sources) + len(expanded)]
        own_ref, other_ref, blocked, placed = refs[len(sources) + len(expanded) + 1 :]
        place(blocked, table_ref, source_refs, size)
        placed[...] = blocked[...].reshape(sequences, depth)
        for side in range(0, total, block):
            value = 0.0
            at = 0
            for expanded_ref in expanded_refs:
                high = expanded_ref.shape[0]
                value = value + jnp.dot(
                    placed[:, at : at + high],
                    expanded_ref[:, side : side + block],
                    preferred_element_type=jnp.float32,
                )
                at += high
            value = value * inverse
            own_ref[:, side : side + block] = value[:part]
            other_ref[:, side : side + block] = value[part:]

    half = jax.ShapeDtypeStruct((part, total), jnp.float32)
    return pl.pallas_call(
        body,
        in_specs=[TABLE] + [WHOLE] * (len(sources) + len(expanded) + 1),
        out_specs=[WHOLE] * 2,
        out_shape=[half, half],
        scratch_shapes=[pltpu.VMEM((count, size, depth), jnp.bfloat16), pltpu.VMEM((sequences, depth), jnp.bfloat16)],
        compiler_params=params(),
        cost_estimate=pl.CostEstimate(flops=2 * sequences * depth * total, transcendentals=0, bytes_accessed=1 << 20),
        name="right_partial",
    )(table, *sources, *expanded, after)


def moved(value, axis, distance):
    size = lax.axis_size(axis)
    return lax.ppermute(value, axis, [(k, (k + distance) % size) for k in range(size)])


def swapped(value, axis, bit):
    return lax.ppermute(value, axis, [(k, k ^ bit) for k in range(lax.axis_size(axis))])


def orders(blocks):
    z_lo, x, core, y, z_hi = (lax.axis_index(name) for name in ROW + COL)
    at = lax.iota(jnp.int32, blocks)
    block = (z_lo ^ (at % 2)) * 8 + (x - at // 2) % 4 * 2 + (core ^ (at // 8))
    left_table = (block // 4 - y) % 4 * 4 + (block - z_hi) % 4
    block = (y - at // 4) % 4 * 4 + (z_hi ^ (at % 4))
    right_table = (block - core) % 2 * 8 + (block // 2 - x) % 4 * 2 + (block // 8 - z_lo) % 2
    return left_table, right_table


def on_device(left_factor, right_factor, pair_grad, projection):
    shared, channels, rows = left_factor.shape
    held, entries, cols = right_factor.shape
    left_flat = jnp.transpose(left_factor, (0, 2, 1)).reshape(shared, rows * channels)
    right_flat = right_factor.reshape(held, entries * cols)
    weights = jnp.swapaxes(projection.reshape(channels, entries, -1), 0, 1).reshape(projection.shape)

    blocks = 4 * 4
    inverse = 1.0 / (blocks * shared)
    left_table, right_table = orders(blocks)
    left_table, right_table, weights = lax.optimization_barrier((left_table, right_table, weights))

    from_z = swapped(right_flat, "z_lo", 1)
    from_hi = swapped(left_flat, "z_hi", 1)
    piece, token, pair_grad = expand(pair_grad, weights, channels, 0)
    expanded = [piece]
    near_right, near_left, token = join([[right_flat, from_z], [left_flat, from_hi]], [token])
    from_x = [moved(near_right, "x", d) for d in (1, 2, 3)]
    from_hi = swapped(near_left, "z_hi", 2)
    for number in (1, 2):
        piece, token = expand(pair_grad, weights, channels, number, [token])
        expanded.append(piece)
    along_x, along_z, token = join([[near_right, *from_x], [near_left, from_hi]], [token])
    right_sources = [along_x, swapped(along_x, "core", 1)]
    left_sources = [along_z] + [moved(along_z, "y", d) for d in (1, 2, 3)]
    expanded.append(expand(pair_grad, weights, channels, 3, [token])[0])

    token, own, *others = left_partial(left_table, right_sources, expanded, held, inverse)
    right_own, right_other = right_partial(right_table, left_sources, expanded, shared, inverse, token)

    left_sum = own
    for d, other in enumerate(others):
        left_sum = left_sum + moved(other, "y", d + 1).astype(jnp.float32)
    left_grad = left_sum[:shared]
    for d in (1, 2, 3):
        piece = left_sum[d * shared : (d + 1) * shared].astype(jnp.bfloat16)
        left_grad = left_grad + moved(piece, "z_hi", d).astype(jnp.float32)
    left_grad = jnp.swapaxes(left_grad.reshape(shared, rows, channels), 1, 2)

    right_sum = right_own + swapped(right_other, "core", 1)
    part = 2 * held
    right_near = right_sum[:part]
    for d in (1, 2, 3):
        piece = right_sum[d * part : (d + 1) * part].astype(jnp.bfloat16)
        right_near = right_near + moved(piece, "x", d).astype(jnp.float32)
    right_grad = right_near[:held] + swapped(right_near[held:].astype(jnp.bfloat16), "z_lo", 1).astype(jnp.float32)
    return (left_grad, right_grad.reshape(held, entries, cols))


def solution(mesh):
    names = ("z_lo", "x", "core", "y", "z_hi")
    torus = Mesh(mesh.devices.reshape(2, 4, 2, 4, 4), names)
    return jax.shard_map(
        on_device,
        mesh=torus,
        in_specs=(P(COL, None, ROW), P(ROW, None, COL), P(ROW, None, COL), P()),
        out_specs=(P(COL, None, ROW), P(ROW, None, COL)),
        check_vma=False,
    )
```

```python
import jax
import jax.numpy as jnp
from jax import lax
from jax.experimental import pallas as pl
from jax.experimental.pallas import tpu as pltpu
from jax.sharding import Mesh
from jax.sharding import PartitionSpec as P

ROW = ("z_lo", "x", "core")
COL = ("y", "z_hi")
VMEM = 12 << 20
PIECES = 4
WHOLE = pl.BlockSpec(memory_space=pltpu.VMEM)
TABLE = pl.BlockSpec(memory_space=pltpu.SMEM)


def params():
    return pltpu.CompilerParams(vmem_limit_bytes=VMEM)


def expand(pair_grad, weights, channels, number, after=()):
    rows, width, cols = pair_grad.shape
    wide = weights.shape[0]
    entries = wide // channels
    held = rows // PIECES
    step = 2
    chunk = 8
    first = number == 0

    def body(weight_ref, grad_ref, *rest):
        out_ref, token_ref, *rest = rest[len(after) :]
        copies = []
        if first:
            source_ref = grad_ref
            grad_ref, sems = rest
            for k in range(rows // chunk):
                part = pl.ds(k * chunk, chunk)
                copies.append(pltpu.make_async_copy(source_ref.at[part], grad_ref.at[part], sems.at[k]))
                copies[k].start()
        for t in range(held // 2):
            if first and t * 2 % chunk == 0:
                copies[t * 2 // chunk].wait()
            i = number * held + t * 2
            pair = jnp.concatenate([grad_ref[i], grad_ref[i + 1]], axis=1)
            base = t * 2 * channels
            for entry in range(0, entries, step):
                piece = weight_ref[entry * channels : (entry + step) * channels, :]
                value = jnp.dot(piece, pair, preferred_element_type=jnp.float32).astype(jnp.bfloat16)
                for k in range(step):
                    block = value[k * channels : (k + 1) * channels]
                    stacked = jnp.concatenate([block[:, :cols], block[:, cols:]], axis=0)
                    side = (entry + k) * cols
                    out_ref[base : base + 2 * channels, side : side + cols] = stacked
        for copy in copies[held // chunk :]:
            copy.wait()
        token_ref[...] = out_ref[:16, :128]

    moved_shape = pltpu.VMEM(pair_grad.shape, pair_grad.dtype)
    return pl.pallas_call(
        body,
        in_specs=[WHOLE, pl.BlockSpec(memory_space=pltpu.HBM) if first else WHOLE] + [WHOLE] * len(after),
        out_specs=[WHOLE] * (3 if first else 2),
        out_shape=[
            pltpu.VMEM((held * channels, entries * cols), jnp.bfloat16),
            jax.ShapeDtypeStruct((16, 128), jnp.bfloat16),
        ]
        + ([moved_shape] if first else []),
        scratch_shapes=[pltpu.SemaphoreType.DMA((rows // chunk,))] if first else [],
        compiler_params=params(),
        cost_estimate=pl.CostEstimate(flops=4 * held * wide * width * cols, transcendentals=0, bytes_accessed=1 << 20),
        name="expand",
    )(weights, pair_grad, *after)


def join(groups, after):
    parts = [part for group in groups for part in group]

    def body(*refs):
        source_refs = refs[: len(parts)]
        out_refs = refs[len(parts) + len(after) : -1]
        at = 0
        for group, out_ref in zip(groups, out_refs):
            top = 0
            for part in group:
                out_ref[top : top + part.shape[0], :] = source_refs[at][...]
                top += part.shape[0]
                at += 1
        refs[-1][...] = refs[len(parts)][...]

    shapes = [(sum(part.shape[0] for part in group), group[0].shape[1]) for group in groups] + [after[0].shape]
    return pl.pallas_call(
        body,
        in_specs=[WHOLE] * (len(parts) + len(after)),
        out_specs=[WHOLE] * len(shapes),
        out_shape=[jax.ShapeDtypeStruct(shape, jnp.bfloat16) for shape in shapes],
        compiler_params=params(),
        cost_estimate=pl.CostEstimate(flops=0, transcendentals=0, bytes_accessed=1 << 20),
        name="join",
    )(*parts, *after)


def place(scratch, table_ref, sources, size):
    at = 0
    for source in sources:
        for top in range(0, source.shape[0], size):
            scratch[table_ref[at]] = source[top : top + size, :]
            at += 1


def left_partial(table, sources, expanded, size, inverse):
    count = table.shape[0]
    sequences = count * size
    depth = expanded[0].shape[1]
    total = sum(e.shape[0] for e in expanded)
    part = sequences // 4
    block = 512

    def body(table_ref, *refs):
        source_refs = refs[: len(sources)]
        expanded_refs = refs[len(sources) : len(sources) + len(expanded)]
        token_ref, own_ref, *other_refs = refs[len(sources) + len(expanded) : -2]
        placed, turned = refs[-2:]
        place(placed, table_ref, source_refs, size)
        turned[...] = placed[...].reshape(sequences, depth).T
        at = 0
        for expanded_ref in expanded_refs:
            for top in range(0, expanded_ref.shape[0], block):
                value = jnp.dot(
                    expanded_ref[top : top + block, :], turned[...], preferred_element_type=jnp.float32
                )
                value = value.T * inverse
                own_ref[:, at : at + block] = value[:part]
                for k, other_ref in enumerate(other_refs):
                    lower = (k + 1) * part
                    other_ref[:, at : at + block] = value[lower : lower + part].astype(jnp.bfloat16)
                at += block
        token_ref[...] = other_refs[0][:16, :128]

    other = jax.ShapeDtypeStruct((part, total), jnp.bfloat16)
    return pl.pallas_call(
        body,
        in_specs=[TABLE] + [WHOLE] * (len(sources) + len(expanded)),
        out_specs=[WHOLE] * 5,
        out_shape=[
            jax.ShapeDtypeStruct((16, 128), jnp.bfloat16),
            jax.ShapeDtypeStruct((part, total), jnp.float32),
            other,
            other,
            other,
        ],
        scratch_shapes=[pltpu.VMEM((count, size, depth), jnp.bfloat16), pltpu.VMEM((depth, sequences), jnp.bfloat16)],
        compiler_params=params(),
        cost_estimate=pl.CostEstimate(flops=4 * sequences * depth * total, transcendentals=0, bytes_accessed=1 << 20),
        name="left_partial",
    )(table, *sources, *expanded)


def right_partial(table, sources, expanded, size, inverse, after):
    count = table.shape[0]
    sequences = count * size
    depth = sum(e.shape[0] for e in expanded)
    total = expanded[0].shape[1]
    part = sequences // 2
    block = 512

    def body(table_ref, *refs):
        source_refs = refs[: len(sources)]
        expanded_refs = refs[len(sources) : len(sources) + len(expanded)]
        own_ref, other_ref, blocked, placed = refs[len(sources) + len(expanded) + 1 :]
        place(blocked, table_ref, source_refs, size)
        placed[...] = blocked[...].reshape(sequences, depth)
        for side in range(0, total, block):
            value = 0.0
            at = 0
            for expanded_ref in expanded_refs:
                high = expanded_ref.shape[0]
                value = value + jnp.dot(
                    placed[:, at : at + high],
                    expanded_ref[:, side : side + block],
                    preferred_element_type=jnp.float32,
                )
                at += high
            value = value * inverse
            own_ref[:, side : side + block] = value[:part]
            other_ref[:, side : side + block] = value[part:]

    half = jax.ShapeDtypeStruct((part, total), jnp.float32)
    return pl.pallas_call(
        body,
        in_specs=[TABLE] + [WHOLE] * (len(sources) + len(expanded) + 1),
        out_specs=[WHOLE] * 2,
        out_shape=[half, half],
        scratch_shapes=[pltpu.VMEM((count, size, depth), jnp.bfloat16), pltpu.VMEM((sequences, depth), jnp.bfloat16)],
        compiler_params=params(),
        cost_estimate=pl.CostEstimate(flops=2 * sequences * depth * total, transcendentals=0, bytes_accessed=1 << 20),
        name="right_partial",
    )(table, *sources, *expanded, after)


def split_sum(own, others, part, after=()):
    rows, width = own.shape
    count = rows // part

    def body(*refs):
        given = refs[: 1 + len(others)]
        token_ref, near_ref, *piece_refs = refs[1 + len(others) + len(after) :]
        total = given[0][...]
        for ref in given[1:]:
            total = total + ref[...].astype(jnp.float32)
        near_ref[...] = total[:part]
        for k, piece_ref in enumerate(piece_refs):
            piece_ref[...] = total[(k + 1) * part : (k + 2) * part].astype(jnp.bfloat16)
        token_ref[...] = total[:8, :128]

    return pl.pallas_call(
        body,
        in_specs=[WHOLE] * (1 + len(others) + len(after)),
        out_specs=[WHOLE] * (1 + count),
        out_shape=[jax.ShapeDtypeStruct((8, 128), jnp.float32), jax.ShapeDtypeStruct((part, width), jnp.float32)]
        + [jax.ShapeDtypeStruct((part, width), jnp.bfloat16)] * (count - 1),
        compiler_params=params(),
        cost_estimate=pl.CostEstimate(flops=0, transcendentals=0, bytes_accessed=1 << 20),
        name="split_sum",
    )(own, *others, *after)


def moved(value, axis, distance):
    size = lax.axis_size(axis)
    return lax.ppermute(value, axis, [(k, (k + distance) % size) for k in range(size)])


def swapped(value, axis, bit):
    return lax.ppermute(value, axis, [(k, k ^ bit) for k in range(lax.axis_size(axis))])


def orders(blocks):
    z_lo, x, core, y, z_hi = (lax.axis_index(name) for name in ROW + COL)
    at = lax.iota(jnp.int32, blocks)
    block = (z_lo ^ (at % 2)) * 8 + (x - at // 2) % 4 * 2 + (core ^ (at // 8))
    left_table = (block // 4 - y) % 4 * 4 + (block - z_hi) % 4
    block = (y - at // 4) % 4 * 4 + (z_hi ^ (at % 4))
    right_table = (block - core) % 2 * 8 + (block // 2 - x) % 4 * 2 + (block // 8 - z_lo) % 2
    return left_table, right_table


def on_device(left_factor, right_factor, pair_grad, projection):
    shared, channels, rows = left_factor.shape
    held, entries, cols = right_factor.shape
    left_flat = jnp.transpose(left_factor, (0, 2, 1)).reshape(shared, rows * channels)
    right_flat = right_factor.reshape(held, entries * cols)
    weights = jnp.swapaxes(projection.reshape(channels, entries, -1), 0, 1).reshape(projection.shape)

    blocks = 4 * 4
    inverse = 1.0 / (blocks * shared)
    left_table, right_table = orders(blocks)
    left_table, right_table, weights = lax.optimization_barrier((left_table, right_table, weights))

    from_z = swapped(right_flat, "z_lo", 1)
    from_hi = swapped(left_flat, "z_hi", 1)
    pair_grad = pltpu.with_memory_space_constraint(pair_grad, pltpu.HBM)
    piece, token, pair_grad = expand(pair_grad, weights, channels, 0)
    expanded = [piece]
    near_right, near_left, token = join([[right_flat, from_z], [left_flat, from_hi]], [token])
    from_x = [moved(near_right, "x", d) for d in (1, 2, 3)]
    from_hi = swapped(near_left, "z_hi", 2)
    for number in (1, 2):
        piece, token = expand(pair_grad, weights, channels, number, [token])
        expanded.append(piece)
    along_x, along_z, token = join([[near_right, *from_x], [near_left, from_hi]], [token])
    right_sources = [along_x, swapped(along_x, "core", 1)]
    left_sources = [along_z] + [moved(along_z, "y", d) for d in (1, 2, 3)]
    expanded.append(expand(pair_grad, weights, channels, 3, [token])[0])

    token, own, *others = left_partial(left_table, right_sources, expanded, held, inverse)
    right_own, right_other = right_partial(right_table, left_sources, expanded, shared, inverse, token)

    left_terms = [moved(other, "y", d + 1) for d, other in enumerate(others)]
    token, right_near, *pieces = split_sum(right_own, [swapped(right_other, "core", 1)], 2 * held)
    right_terms = [moved(piece, "x", d + 1) for d, piece in enumerate(pieces)]
    token, left_grad, *pieces = split_sum(own, left_terms, shared, [token])
    for d, piece in enumerate(pieces):
        left_grad = left_grad + moved(piece, "z_hi", d + 1).astype(jnp.float32)
    left_grad = jnp.swapaxes(left_grad.reshape(shared, rows, channels), 1, 2)

    for term in right_terms:
        right_near = right_near + term.astype(jnp.float32)
    right_grad = right_near[:held] + swapped(right_near[held:].astype(jnp.bfloat16), "z_lo", 1).astype(jnp.float32)
    return (left_grad, right_grad.reshape(held, entries, cols))


def solution(mesh):
    names = ("z_lo", "x", "core", "y", "z_hi")
    torus = Mesh(mesh.devices.reshape(2, 4, 2, 4, 4), names)
    return jax.shard_map(
        on_device,
        mesh=torus,
        in_specs=(P(COL, None, ROW), P(ROW, None, COL), P(ROW, None, COL), P()),
        out_specs=(P(COL, None, ROW), P(ROW, None, COL)),
        check_vma=False,
    )
```

```python
import jax
import jax.numpy as jnp
from jax import lax
from jax.experimental import pallas as pl
from jax.experimental.pallas import tpu as pltpu
from jax.sharding import Mesh
from jax.sharding import PartitionSpec as P

ROW = ("z_lo", "x", "core")
COL = ("y", "z_hi")
VMEM = 12 << 20
PIECES = 4
WHOLE = pl.BlockSpec(memory_space=pltpu.VMEM)
TABLE = pl.BlockSpec(memory_space=pltpu.SMEM)


def params():
    return pltpu.CompilerParams(vmem_limit_bytes=VMEM)


def expand(pair_grad, weights, channels, number, after=()):
    rows, width, cols = pair_grad.shape
    wide = weights.shape[0]
    entries = wide // channels
    held = rows // PIECES
    step = 2
    chunk = 8
    first = number == 0

    def body(weight_ref, grad_ref, *rest):
        out_ref, token_ref, *rest = rest[len(after) :]
        copies = []
        if first:
            source_ref = grad_ref
            grad_ref, sems = rest
            for k in range(rows // chunk):
                part = pl.ds(k * chunk, chunk)
                copies.append(pltpu.make_async_copy(source_ref.at[part], grad_ref.at[part], sems.at[k]))
                copies[k].start()
        for t in range(held // 2):
            if first and t * 2 % chunk == 0:
                copies[t * 2 // chunk].wait()
            i = number * held + t * 2
            pair = jnp.concatenate([grad_ref[i], grad_ref[i + 1]], axis=1)
            base = t * 2 * channels
            for entry in range(0, entries, step):
                piece = weight_ref[entry * channels : (entry + step) * channels, :]
                value = jnp.dot(piece, pair, preferred_element_type=jnp.float32).astype(jnp.bfloat16)
                for k in range(step):
                    block = value[k * channels : (k + 1) * channels]
                    stacked = jnp.concatenate([block[:, :cols], block[:, cols:]], axis=0)
                    side = (entry + k) * cols
                    out_ref[base : base + 2 * channels, side : side + cols] = stacked
        for copy in copies[held // chunk :]:
            copy.wait()
        token_ref[...] = out_ref[:16, :128]

    moved_shape = pltpu.VMEM(pair_grad.shape, pair_grad.dtype)
    return pl.pallas_call(
        body,
        in_specs=[WHOLE, pl.BlockSpec(memory_space=pltpu.HBM) if first else WHOLE] + [WHOLE] * len(after),
        out_specs=[WHOLE] * (3 if first else 2),
        out_shape=[
            pltpu.VMEM((held * channels, entries * cols), jnp.bfloat16),
            jax.ShapeDtypeStruct((16, 128), jnp.bfloat16),
        ]
        + ([moved_shape] if first else []),
        scratch_shapes=[pltpu.SemaphoreType.DMA((rows // chunk,))] if first else [],
        compiler_params=params(),
        cost_estimate=pl.CostEstimate(flops=4 * held * wide * width * cols, transcendentals=0, bytes_accessed=1 << 20),
        name="expand",
    )(weights, pair_grad, *after)


def join(groups, after):
    parts = [part for group in groups for part in group]

    def body(*refs):
        source_refs = refs[: len(parts)]
        out_refs = refs[len(parts) + len(after) : -1]
        at = 0
        for group, out_ref in zip(groups, out_refs):
            top = 0
            for part in group:
                out_ref[top : top + part.shape[0], :] = source_refs[at][...]
                top += part.shape[0]
                at += 1
        refs[-1][...] = refs[len(parts)][...]

    shapes = [(sum(part.shape[0] for part in group), group[0].shape[1]) for group in groups] + [after[0].shape]
    return pl.pallas_call(
        body,
        in_specs=[WHOLE] * (len(parts) + len(after)),
        out_specs=[WHOLE] * len(shapes),
        out_shape=[jax.ShapeDtypeStruct(shape, jnp.bfloat16) for shape in shapes],
        compiler_params=params(),
        cost_estimate=pl.CostEstimate(flops=0, transcendentals=0, bytes_accessed=1 << 20),
        name="join",
    )(*parts, *after)


def place(scratch, table_ref, sources, size):
    at = 0
    for source in sources:
        for top in range(0, source.shape[0], size):
            scratch[table_ref[at]] = source[top : top + size, :]
            at += 1


def left_partial(table, sources, expanded, size, inverse):
    count = table.shape[0]
    sequences = count * size
    depth = expanded[0].shape[1]
    total = sum(e.shape[0] for e in expanded)
    part = sequences // 4
    block = 512

    def body(table_ref, *refs):
        source_refs = refs[: len(sources)]
        expanded_refs = refs[len(sources) : len(sources) + len(expanded)]
        token_ref, own_ref, *other_refs = refs[len(sources) + len(expanded) : -2]
        placed, turned = refs[-2:]
        place(placed, table_ref, source_refs, size)
        turned[...] = placed[...].reshape(sequences, depth).T
        at = 0
        for expanded_ref in expanded_refs:
            for top in range(0, expanded_ref.shape[0], block):
                value = jnp.dot(
                    expanded_ref[top : top + block, :], turned[...], preferred_element_type=jnp.float32
                )
                value = value.T * inverse
                own_ref[:, at : at + block] = value[:part]
                for k, other_ref in enumerate(other_refs):
                    lower = (k + 1) * part
                    other_ref[:, at : at + block] = value[lower : lower + part].astype(jnp.bfloat16)
                at += block
        token_ref[...] = other_refs[0][:16, :128]

    other = jax.ShapeDtypeStruct((part, total), jnp.bfloat16)
    return pl.pallas_call(
        body,
        in_specs=[TABLE] + [WHOLE] * (len(sources) + len(expanded)),
        out_specs=[WHOLE] * 5,
        out_shape=[
            jax.ShapeDtypeStruct((16, 128), jnp.bfloat16),
            jax.ShapeDtypeStruct((part, total), jnp.float32),
            other,
            other,
            other,
        ],
        scratch_shapes=[pltpu.VMEM((count, size, depth), jnp.bfloat16), pltpu.VMEM((depth, sequences), jnp.bfloat16)],
        compiler_params=params(),
        cost_estimate=pl.CostEstimate(flops=4 * sequences * depth * total, transcendentals=0, bytes_accessed=1 << 20),
        name="left_partial",
    )(table, *sources, *expanded)


def right_partial(table, sources, expanded, size, inverse, after):
    count = table.shape[0]
    sequences = count * size
    depth = sum(e.shape[0] for e in expanded)
    total = expanded[0].shape[1]
    part = sequences // 2
    block = 512

    def body(table_ref, *refs):
        source_refs = refs[: len(sources)]
        expanded_refs = refs[len(sources) : len(sources) + len(expanded)]
        own_ref, other_ref, blocked, placed = refs[len(sources) + len(expanded) + 1 :]
        place(blocked, table_ref, source_refs, size)
        placed[...] = blocked[...].reshape(sequences, depth)
        for side in range(0, total, block):
            value = 0.0
            at = 0
            for expanded_ref in expanded_refs:
                high = expanded_ref.shape[0]
                value = value + jnp.dot(
                    placed[:, at : at + high],
                    expanded_ref[:, side : side + block],
                    preferred_element_type=jnp.float32,
                )
                at += high
            value = value * inverse
            own_ref[:, side : side + block] = value[:part]
            other_ref[:, side : side + block] = value[part:]

    half = jax.ShapeDtypeStruct((part, total), jnp.float32)
    return pl.pallas_call(
        body,
        in_specs=[TABLE] + [WHOLE] * (len(sources) + len(expanded) + 1),
        out_specs=[WHOLE] * 2,
        out_shape=[half, half],
        scratch_shapes=[pltpu.VMEM((count, size, depth), jnp.bfloat16), pltpu.VMEM((sequences, depth), jnp.bfloat16)],
        compiler_params=params(),
        cost_estimate=pl.CostEstimate(flops=2 * sequences * depth * total, transcendentals=0, bytes_accessed=1 << 20),
        name="right_partial",
    )(table, *sources, *expanded, after)


def moved(value, axis, distance):
    size = lax.axis_size(axis)
    return lax.ppermute(value, axis, [(k, (k + distance) % size) for k in range(size)])


def swapped(value, axis, bit):
    return lax.ppermute(value, axis, [(k, k ^ bit) for k in range(lax.axis_size(axis))])


def orders(blocks):
    z_lo, x, core, y, z_hi = (lax.axis_index(name) for name in ROW + COL)
    at = lax.iota(jnp.int32, blocks)
    block = (z_lo ^ (at % 2)) * 8 + (x - at // 2) % 4 * 2 + (core ^ (at // 8))
    left_table = (block // 4 - y) % 4 * 4 + (block - z_hi) % 4
    step = at % 4
    block = (y - at // 4) % 4 * 4 + (z_hi - jnp.where(step == 2, 3, jnp.where(step == 3, 2, step))) % 4
    right_table = (block - core) % 2 * 8 + (block // 2 - x) % 4 * 2 + (block // 8 - z_lo) % 2
    return left_table, right_table


def on_device(left_factor, right_factor, pair_grad, projection):
    shared, channels, rows = left_factor.shape
    held, entries, cols = right_factor.shape
    left_flat = jnp.transpose(left_factor, (0, 2, 1)).reshape(shared, rows * channels)
    right_flat = right_factor.reshape(held, entries * cols)
    weights = jnp.swapaxes(projection.reshape(channels, entries, -1), 0, 1).reshape(projection.shape)

    blocks = 4 * 4
    inverse = 1.0 / (blocks * shared)
    left_table, right_table = orders(blocks)
    left_table, right_table, weights = lax.optimization_barrier((left_table, right_table, weights))

    from_z = swapped(right_flat, "z_lo", 1)
    from_hi = [moved(left_flat, "z_hi", d) for d in (1, -1)]
    pair_grad = pltpu.with_memory_space_constraint(pair_grad, pltpu.HBM)
    piece, token, pair_grad = expand(pair_grad, weights, channels, 0)
    expanded = [piece]
    near_right, near_left, token = join([[right_flat, from_z], [left_flat, *from_hi]], [token])
    from_x = [moved(near_right, "x", d) for d in (1, 2, 3)]
    from_hi = moved(from_hi[0], "z_hi", 1)
    for number in (1, 2):
        piece, token = expand(pair_grad, weights, channels, number, [token])
        expanded.append(piece)
    along_x, along_z, token = join([[near_right, *from_x], [near_left, from_hi]], [token])
    right_sources = [along_x, swapped(along_x, "core", 1)]
    left_sources = [along_z] + [moved(along_z, "y", d) for d in (1, 2, 3)]
    expanded.append(expand(pair_grad, weights, channels, 3, [token])[0])

    token, own, *others = left_partial(left_table, right_sources, expanded, held, inverse)
    right_own, right_other = right_partial(right_table, left_sources, expanded, shared, inverse, token)

    left_sum = own
    for d, other in enumerate(others):
        left_sum = left_sum + moved(other, "y", d + 1).astype(jnp.float32)
    nearest, next_one, opposite, last = (left_sum[d * shared : (d + 1) * shared] for d in range(4))
    from_next = moved(last.astype(jnp.bfloat16), "z_hi", -1)
    passed = moved(opposite.astype(jnp.bfloat16), "z_hi", 1)
    passed = moved((next_one + passed.astype(jnp.float32)).astype(jnp.bfloat16), "z_hi", 1)
    left_grad = nearest + from_next.astype(jnp.float32) + passed.astype(jnp.float32)
    left_grad = jnp.swapaxes(left_grad.reshape(shared, rows, channels), 1, 2)

    right_sum = right_own + swapped(right_other, "core", 1)
    part = 2 * held
    right_near = right_sum[:part]
    for d in (1, 2, 3):
        piece = right_sum[d * part : (d + 1) * part].astype(jnp.bfloat16)
        right_near = right_near + moved(piece, "x", d).astype(jnp.float32)
    right_grad = right_near[:held] + swapped(right_near[held:].astype(jnp.bfloat16), "z_lo", 1).astype(jnp.float32)
    return (left_grad, right_grad.reshape(held, entries, cols))


def solution(mesh):
    names = ("z_lo", "x", "core", "y", "z_hi")
    torus = Mesh(mesh.devices.reshape(2, 4, 2, 4, 4), names)
    return jax.shard_map(
        on_device,
        mesh=torus,
        in_specs=(P(COL, None, ROW), P(ROW, None, COL), P(ROW, None, COL), P()),
        out_specs=(P(COL, None, ROW), P(ROW, None, COL)),
        check_vma=False,
    )
```

```python
import jax
import jax.numpy as jnp
from jax import lax
from jax.experimental import pallas as pl
from jax.experimental.pallas import tpu as pltpu
from jax.sharding import Mesh
from jax.sharding import PartitionSpec as P

ROW = ("z_lo", "x", "core")
COL = ("y", "z_hi")
VMEM = 12 << 20
PIECES = 4
WHOLE = pl.BlockSpec(memory_space=pltpu.VMEM)
TABLE = pl.BlockSpec(memory_space=pltpu.SMEM)


def params():
    return pltpu.CompilerParams(vmem_limit_bytes=VMEM)


def expand(pair_grad, weights, channels, number, after=()):
    rows, width, cols = pair_grad.shape
    wide = weights.shape[0]
    entries = wide // channels
    held = rows // PIECES
    step = 2
    chunk = 8
    first = number == 0

    def body(weight_ref, grad_ref, *rest):
        out_ref, token_ref, *rest = rest[len(after) :]
        copies = []
        if first:
            source_ref = grad_ref
            grad_ref, sems = rest
            for k in range(rows // chunk):
                part = pl.ds(k * chunk, chunk)
                copies.append(pltpu.make_async_copy(source_ref.at[part], grad_ref.at[part], sems.at[k]))
                copies[k].start()
        for t in range(held // 2):
            if first and t * 2 % chunk == 0:
                copies[t * 2 // chunk].wait()
            i = number * held + t * 2
            pair = jnp.concatenate([grad_ref[i], grad_ref[i + 1]], axis=1)
            base = t * 2 * channels
            for entry in range(0, entries, step):
                piece = weight_ref[entry * channels : (entry + step) * channels, :]
                value = jnp.dot(piece, pair, preferred_element_type=jnp.float32).astype(jnp.bfloat16)
                for k in range(step):
                    block = value[k * channels : (k + 1) * channels]
                    stacked = jnp.concatenate([block[:, :cols], block[:, cols:]], axis=0)
                    side = (entry + k) * cols
                    out_ref[base : base + 2 * channels, side : side + cols] = stacked
        for copy in copies[held // chunk :]:
            copy.wait()
        token_ref[...] = out_ref[:16, :128]

    moved_shape = pltpu.VMEM(pair_grad.shape, pair_grad.dtype)
    return pl.pallas_call(
        body,
        in_specs=[WHOLE, pl.BlockSpec(memory_space=pltpu.HBM) if first else WHOLE] + [WHOLE] * len(after),
        out_specs=[WHOLE] * (3 if first else 2),
        out_shape=[
            pltpu.VMEM((held * channels, entries * cols), jnp.bfloat16),
            jax.ShapeDtypeStruct((16, 128), jnp.bfloat16),
        ]
        + ([moved_shape] if first else []),
        scratch_shapes=[pltpu.SemaphoreType.DMA((rows // chunk,))] if first else [],
        compiler_params=params(),
        cost_estimate=pl.CostEstimate(flops=4 * held * wide * width * cols, transcendentals=0, bytes_accessed=1 << 20),
        name="expand",
    )(weights, pair_grad, *after)


def join(groups, after):
    parts = [part for group in groups for part in group]

    def body(*refs):
        source_refs = refs[: len(parts)]
        out_refs = refs[len(parts) + len(after) : -1]
        at = 0
        for group, out_ref in zip(groups, out_refs):
            top = 0
            for part in group:
                out_ref[top : top + part.shape[0], :] = source_refs[at][...]
                top += part.shape[0]
                at += 1
        refs[-1][...] = refs[len(parts)][...]

    shapes = [(sum(part.shape[0] for part in group), group[0].shape[1]) for group in groups] + [after[0].shape]
    return pl.pallas_call(
        body,
        in_specs=[WHOLE] * (len(parts) + len(after)),
        out_specs=[WHOLE] * len(shapes),
        out_shape=[jax.ShapeDtypeStruct(shape, jnp.bfloat16) for shape in shapes],
        compiler_params=params(),
        cost_estimate=pl.CostEstimate(flops=0, transcendentals=0, bytes_accessed=1 << 20),
        name="join",
    )(*parts, *after)


def place(scratch, table_ref, sources, size):
    at = 0
    for source in sources:
        for top in range(0, source.shape[0], size):
            scratch[table_ref[at]] = source[top : top + size, :]
            at += 1


def left_partial(table, sources, expanded, size, inverse):
    count = table.shape[0]
    sequences = count * size
    depth = expanded[0].shape[1]
    total = sum(e.shape[0] for e in expanded)
    part = sequences // 4
    block = 512

    def body(table_ref, *refs):
        source_refs = refs[: len(sources)]
        expanded_refs = refs[len(sources) : len(sources) + len(expanded)]
        token_ref, own_ref, *other_refs = refs[len(sources) + len(expanded) : -2]
        placed, turned = refs[-2:]
        place(placed, table_ref, source_refs, size)
        turned[...] = placed[...].reshape(sequences, depth).T
        at = 0
        for expanded_ref in expanded_refs:
            for top in range(0, expanded_ref.shape[0], block):
                value = jnp.dot(
                    expanded_ref[top : top + block, :], turned[...], preferred_element_type=jnp.float32
                )
                value = value.T * inverse
                own_ref[:, at : at + block] = value[:part]
                for k, other_ref in enumerate(other_refs):
                    lower = (k + 1) * part
                    other_ref[:, at : at + block] = value[lower : lower + part].astype(jnp.bfloat16)
                at += block
        token_ref[...] = other_refs[0][:16, :128]

    other = jax.ShapeDtypeStruct((part, total), jnp.bfloat16)
    return pl.pallas_call(
        body,
        in_specs=[TABLE] + [WHOLE] * (len(sources) + len(expanded)),
        out_specs=[WHOLE] * 5,
        out_shape=[
            jax.ShapeDtypeStruct((16, 128), jnp.bfloat16),
            jax.ShapeDtypeStruct((part, total), jnp.float32),
            other,
            other,
            other,
        ],
        scratch_shapes=[pltpu.VMEM((count, size, depth), jnp.bfloat16), pltpu.VMEM((depth, sequences), jnp.bfloat16)],
        compiler_params=params(),
        cost_estimate=pl.CostEstimate(flops=4 * sequences * depth * total, transcendentals=0, bytes_accessed=1 << 20),
        name="left_partial",
    )(table, *sources, *expanded)


def right_partial(table, sources, expanded, size, inverse, after):
    count = table.shape[0]
    sequences = count * size
    depth = sum(e.shape[0] for e in expanded)
    total = expanded[0].shape[1]
    part = sequences // 2
    block = 512

    def body(table_ref, *refs):
        source_refs = refs[: len(sources)]
        expanded_refs = refs[len(sources) : len(sources) + len(expanded)]
        own_ref, other_ref, blocked, placed = refs[len(sources) + len(expanded) + 1 :]
        place(blocked, table_ref, source_refs, size)
        placed[...] = blocked[...].reshape(sequences, depth)
        for side in range(0, total, block):
            value = 0.0
            at = 0
            for expanded_ref in expanded_refs:
                high = expanded_ref.shape[0]
                value = value + jnp.dot(
                    placed[:, at : at + high],
                    expanded_ref[:, side : side + block],
                    preferred_element_type=jnp.float32,
                )
                at += high
            value = value * inverse
            own_ref[:, side : side + block] = value[:part]
            other_ref[:, side : side + block] = value[part:]

    half = jax.ShapeDtypeStruct((part, total), jnp.float32)
    return pl.pallas_call(
        body,
        in_specs=[TABLE] + [WHOLE] * (len(sources) + len(expanded) + 1),
        out_specs=[WHOLE] * 2,
        out_shape=[half, half],
        scratch_shapes=[pltpu.VMEM((count, size, depth), jnp.bfloat16), pltpu.VMEM((sequences, depth), jnp.bfloat16)],
        compiler_params=params(),
        cost_estimate=pl.CostEstimate(flops=2 * sequences * depth * total, transcendentals=0, bytes_accessed=1 << 20),
        name="right_partial",
    )(table, *sources, *expanded, after)


def moved(value, axis, distance):
    size = lax.axis_size(axis)
    return lax.ppermute(value, axis, [(k, (k + distance) % size) for k in range(size)])


def swapped(value, axis, bit):
    return lax.ppermute(value, axis, [(k, k ^ bit) for k in range(lax.axis_size(axis))])


def orders(blocks):
    z_lo, x, core, y, z_hi = (lax.axis_index(name) for name in ROW + COL)
    at = lax.iota(jnp.int32, blocks)
    block = (z_lo ^ (at % 2)) * 8 + (x - at // 2) % 4 * 2 + (core ^ (at // 8))
    left_table = (block // 4 - y) % 4 * 4 + (block - z_hi) % 4
    block = (y - at // 4) % 4 * 4 + (z_hi ^ (at % 4))
    right_table = (block - core) % 2 * 8 + (block // 2 - x) % 4 * 2 + (block // 8 - z_lo) % 2
    return left_table, right_table


def on_device(left_factor, right_factor, pair_grad, projection):
    shared, channels, rows = left_factor.shape
    held, entries, cols = right_factor.shape
    left_flat = jnp.transpose(left_factor, (0, 2, 1)).reshape(shared, rows * channels)
    right_flat = right_factor.reshape(held, entries * cols)
    weights = jnp.swapaxes(projection.reshape(channels, entries, -1), 0, 1).reshape(projection.shape)

    blocks = 4 * 4
    inverse = 1.0 / (blocks * shared)
    left_table, right_table = orders(blocks)
    left_table, right_table, weights = lax.optimization_barrier((left_table, right_table, weights))

    from_z = swapped(right_flat, "z_lo", 1)
    from_hi = swapped(left_flat, "z_hi", 1)
    pair_grad = pltpu.with_memory_space_constraint(pair_grad, pltpu.HBM)
    piece, token, pair_grad = expand(pair_grad, weights, channels, 0)
    expanded = [piece]
    near_right, near_left, token = join([[right_flat, from_z], [left_flat, from_hi]], [token])
    from_x = [moved(near_right, "x", d) for d in (1, 2, 3)]
    from_hi = swapped(near_left, "z_hi", 2)
    for number in (1, 2):
        piece, token = expand(pair_grad, weights, channels, number, [token])
        expanded.append(piece)
    along_x, along_z, token = join([[near_right, *from_x], [near_left, from_hi]], [token])
    right_sources = [along_x, swapped(along_x, "core", 1)]
    left_sources = [along_z] + [moved(along_z, "y", d) for d in (1, 2, 3)]
    expanded.append(expand(pair_grad, weights, channels, 3, [token])[0])

    token, own, *others = left_partial(left_table, right_sources, expanded, held, inverse)
    right_own, right_other = right_partial(right_table, left_sources, expanded, shared, inverse, token)

    left_sum = own
    for d, other in enumerate(others):
        left_sum = left_sum + moved(other, "y", d + 1).astype(jnp.float32)
    nearest, next_one, opposite, last = (left_sum[d * shared : (d + 1) * shared] for d in range(4))
    from_next = moved(last.astype(jnp.bfloat16), "z_hi", -1)
    passed = moved(opposite.astype(jnp.bfloat16), "z_hi", 1)
    passed = moved((next_one + passed.astype(jnp.float32)).astype(jnp.bfloat16), "z_hi", 1)
    left_grad = nearest + from_next.astype(jnp.float32) + passed.astype(jnp.float32)
    left_grad = jnp.swapaxes(left_grad.reshape(shared, rows, channels), 1, 2)

    right_sum = right_own + swapped(right_other, "core", 1)
    part = 2 * held
    right_near = right_sum[:part]
    for d in (1, 2, 3):
        piece = right_sum[d * part : (d + 1) * part].astype(jnp.bfloat16)
        right_near = right_near + moved(piece, "x", d).astype(jnp.float32)
    right_grad = right_near[:held] + swapped(right_near[held:].astype(jnp.bfloat16), "z_lo", 1).astype(jnp.float32)
    return (left_grad, right_grad.reshape(held, entries, cols))


def solution(mesh):
    names = ("z_lo", "x", "core", "y", "z_hi")
    torus = Mesh(mesh.devices.reshape(2, 4, 2, 4, 4), names)
    return jax.shard_map(
        on_device,
        mesh=torus,
        in_specs=(P(COL, None, ROW), P(ROW, None, COL), P(ROW, None, COL), P()),
        out_specs=(P(COL, None, ROW), P(ROW, None, COL)),
        check_vma=False,
    )
```

```python
import jax
import jax.numpy as jnp
from jax import lax
from jax.experimental import pallas as pl
from jax.experimental.pallas import tpu as pltpu
from jax.sharding import Mesh
from jax.sharding import PartitionSpec as P

ROW = ("z_lo", "x", "core")
COL = ("y", "z_hi")
VMEM = 12 << 20
PIECES = 4
PARTS = 1
WHOLE = pl.BlockSpec(memory_space=pltpu.VMEM)
TABLE = pl.BlockSpec(memory_space=pltpu.SMEM)


def params():
    return pltpu.CompilerParams(vmem_limit_bytes=VMEM)


def expand(pair_grad, weights, channels, number, after=()):
    rows, width, cols = pair_grad.shape
    wide = weights.shape[0]
    entries = wide // channels
    held = rows // PIECES
    step = 2
    chunk = 8
    first = number == 0

    def body(weight_ref, grad_ref, *rest):
        out_ref, token_ref, *rest = rest[len(after) :]
        copies = []
        if first:
            source_ref = grad_ref
            grad_ref, sems = rest
            for k in range(rows // chunk):
                part = pl.ds(k * chunk, chunk)
                copies.append(pltpu.make_async_copy(source_ref.at[part], grad_ref.at[part], sems.at[k]))
                copies[k].start()
        for t in range(held // 2):
            if first and t * 2 % chunk == 0:
                copies[t * 2 // chunk].wait()
            i = number * held + t * 2
            pair = jnp.concatenate([grad_ref[i], grad_ref[i + 1]], axis=1)
            base = t * 2 * channels
            for entry in range(0, entries, step):
                piece = weight_ref[entry * channels : (entry + step) * channels, :]
                value = jnp.dot(piece, pair, preferred_element_type=jnp.float32).astype(jnp.bfloat16)
                for k in range(step):
                    block = value[k * channels : (k + 1) * channels]
                    stacked = jnp.concatenate([block[:, :cols], block[:, cols:]], axis=0)
                    side = (entry + k) * cols
                    out_ref[base : base + 2 * channels, side : side + cols] = stacked
        for copy in copies[held // chunk :]:
            copy.wait()
        token_ref[...] = out_ref[:16, :128]

    moved_shape = pltpu.VMEM(pair_grad.shape, pair_grad.dtype)
    return pl.pallas_call(
        body,
        in_specs=[WHOLE, pl.BlockSpec(memory_space=pltpu.HBM) if first else WHOLE] + [WHOLE] * len(after),
        out_specs=[WHOLE] * (3 if first else 2),
        out_shape=[
            pltpu.VMEM((held * channels, entries * cols), jnp.bfloat16),
            jax.ShapeDtypeStruct((16, 128), jnp.bfloat16),
        ]
        + ([moved_shape] if first else []),
        scratch_shapes=[pltpu.SemaphoreType.DMA((rows // chunk,))] if first else [],
        compiler_params=params(),
        cost_estimate=pl.CostEstimate(flops=4 * held * wide * width * cols, transcendentals=0, bytes_accessed=1 << 20),
        name="expand",
    )(weights, pair_grad, *after)


def join(groups, after):
    parts = [part for group in groups for part in group]

    def body(*refs):
        source_refs = refs[: len(parts)]
        out_refs = refs[len(parts) + len(after) : -1]
        at = 0
        for group, out_ref in zip(groups, out_refs):
            top = 0
            for part in group:
                out_ref[top : top + part.shape[0], :] = source_refs[at][...]
                top += part.shape[0]
                at += 1
        refs[-1][...] = refs[len(parts)][...]

    shapes = [(sum(part.shape[0] for part in group), group[0].shape[1]) for group in groups] + [after[0].shape]
    return pl.pallas_call(
        body,
        in_specs=[WHOLE] * (len(parts) + len(after)),
        out_specs=[WHOLE] * len(shapes),
        out_shape=[jax.ShapeDtypeStruct(shape, jnp.bfloat16) for shape in shapes],
        compiler_params=params(),
        cost_estimate=pl.CostEstimate(flops=0, transcendentals=0, bytes_accessed=1 << 20),
        name="join",
    )(*parts, *after)


def place(scratch, table_ref, sources, size):
    at = 0
    for source in sources:
        for top in range(0, source.shape[0], size):
            scratch[table_ref[at]] = source[top : top + size, :]
            at += 1


def left_partial(table, sources, expanded, size, inverse):
    count = table.shape[0]
    sequences = count * size
    depth = expanded[0].shape[1]
    total = sum(e.shape[0] for e in expanded)
    part = sequences // 4
    block = 512

    def body(table_ref, *refs):
        source_refs = refs[: len(sources)]
        expanded_refs = refs[len(sources) : len(sources) + len(expanded)]
        token_ref, own_ref, *other_refs = refs[len(sources) + len(expanded) : -2]
        placed, turned = refs[-2:]
        place(placed, table_ref, source_refs, size)
        turned[...] = placed[...].reshape(sequences, depth).T
        at = 0
        for expanded_ref in expanded_refs:
            for top in range(0, expanded_ref.shape[0], block):
                value = jnp.dot(
                    expanded_ref[top : top + block, :], turned[...], preferred_element_type=jnp.float32
                )
                value = value.T * inverse
                own_ref[:, at : at + block] = value[:part]
                for k, other_ref in enumerate(other_refs):
                    lower = (k + 1) * part
                    other_ref[:, at : at + block] = value[lower : lower + part].astype(jnp.bfloat16)
                at += block
        token_ref[...] = other_refs[0][:16, :128]

    other = jax.ShapeDtypeStruct((part, total), jnp.bfloat16)
    return pl.pallas_call(
        body,
        in_specs=[TABLE] + [WHOLE] * (len(sources) + len(expanded)),
        out_specs=[WHOLE] * 5,
        out_shape=[
            jax.ShapeDtypeStruct((16, 128), jnp.bfloat16),
            jax.ShapeDtypeStruct((part, total), jnp.float32),
            other,
            other,
            other,
        ],
        scratch_shapes=[pltpu.VMEM((count, size, depth), jnp.bfloat16), pltpu.VMEM((depth, sequences), jnp.bfloat16)],
        compiler_params=params(),
        cost_estimate=pl.CostEstimate(flops=4 * sequences * depth * total, transcendentals=0, bytes_accessed=1 << 20),
        name="left_partial",
    )(table, *sources, *expanded)


def right_partial(table, sources, expanded, size, inverse, after):
    count = table.shape[0]
    sequences = count * size
    depth = sum(e.shape[0] for e in expanded)
    total = expanded[0].shape[1]
    part = sequences // 2
    block = 512

    def body(table_ref, *refs):
        source_refs = refs[: len(sources)]
        expanded_refs = refs[len(sources) : len(sources) + len(expanded)]
        own_ref, *other_refs, blocked, placed = refs[len(sources) + len(expanded) + 1 :]
        place(blocked, table_ref, source_refs, size)
        placed[...] = blocked[...].reshape(sequences, depth)
        for side in range(0, total, block):
            value = 0.0
            at = 0
            for expanded_ref in expanded_refs:
                high = expanded_ref.shape[0]
                value = value + jnp.dot(
                    placed[:, at : at + high],
                    expanded_ref[:, side : side + block],
                    preferred_element_type=jnp.float32,
                )
                at += high
            value = value * inverse
            own_ref[:, side : side + block] = value[:part]
            for k, other_ref in enumerate(other_refs):
                lower = part + k * (part // PARTS)
                other_ref[:, side : side + block] = value[lower : lower + part // PARTS].astype(other_ref.dtype)

    half = jax.ShapeDtypeStruct((part, total), jnp.float32)
    other = jax.ShapeDtypeStruct((part // PARTS, total), jnp.float32)
    return pl.pallas_call(
        body,
        in_specs=[TABLE] + [WHOLE] * (len(sources) + len(expanded) + 1),
        out_specs=[WHOLE] * (1 + PARTS),
        out_shape=[half] + [other] * PARTS,
        scratch_shapes=[pltpu.VMEM((count, size, depth), jnp.bfloat16), pltpu.VMEM((sequences, depth), jnp.bfloat16)],
        compiler_params=params(),
        cost_estimate=pl.CostEstimate(flops=2 * sequences * depth * total, transcendentals=0, bytes_accessed=1 << 20),
        name="right_partial",
    )(table, *sources, *expanded, after)


def column_sum(own, others, part, after):
    width = own.shape[1]

    def body(own_ref, *refs):
        total = own_ref[...]
        for ref in refs[: len(others)]:
            total = total + ref[...].astype(jnp.float32)
        for k, out_ref in enumerate(refs[len(others) + 1 :]):
            out_ref[...] = total[k * part : (k + 1) * part].astype(out_ref.dtype)

    return pl.pallas_call(
        body,
        in_specs=[WHOLE] * (2 + len(others)),
        out_specs=[WHOLE] * 4,
        out_shape=[jax.ShapeDtypeStruct((part, width), jnp.float32)] * 2
        + [jax.ShapeDtypeStruct((part, width), jnp.bfloat16)] * 2,
        compiler_params=params(),
        cost_estimate=pl.CostEstimate(flops=0, transcendentals=0, bytes_accessed=0),
        name="column_sum",
    )(own, *others, after)


def split_sum(own, others, part, after=(), stacked=False):
    rows, width = own.shape
    count = rows // part

    def body(*refs):
        given = refs[: 1 + len(others)]
        token_ref, near_ref, *piece_refs = refs[1 + len(others) + len(after) :]
        total = given[0][...]
        terms = [ref[...].astype(jnp.float32) for ref in given[1:]]
        if stacked:
            terms = [jnp.concatenate(terms, axis=0)]
        for term in terms:
            total = total + term
        near_ref[...] = total[:part]
        for k, piece_ref in enumerate(piece_refs):
            piece_ref[...] = total[(k + 1) * part : (k + 2) * part].astype(jnp.bfloat16)
        token_ref[...] = total[:8, :128]

    return pl.pallas_call(
        body,
        in_specs=[WHOLE] * (1 + len(others) + len(after)),
        out_specs=[WHOLE] * (1 + count),
        out_shape=[jax.ShapeDtypeStruct((8, 128), jnp.float32), jax.ShapeDtypeStruct((part, width), jnp.float32)]
        + [jax.ShapeDtypeStruct((part, width), jnp.bfloat16)] * (count - 1),
        compiler_params=params(),
        cost_estimate=pl.CostEstimate(flops=0, transcendentals=0, bytes_accessed=0),
        name="split_sum",
    )(own, *others, *after)


def moved(value, axis, distance):
    size = lax.axis_size(axis)
    return lax.ppermute(value, axis, [(k, (k + distance) % size) for k in range(size)])


def swapped(value, axis, bit):
    return lax.ppermute(value, axis, [(k, k ^ bit) for k in range(lax.axis_size(axis))])


def orders(blocks):
    z_lo, x, core, y, z_hi = (lax.axis_index(name) for name in ROW + COL)
    at = lax.iota(jnp.int32, blocks)
    block = (z_lo ^ (at % 2)) * 8 + (x - at // 2) % 4 * 2 + (core ^ (at // 8))
    left_table = (block // 4 - y) % 4 * 4 + (block - z_hi) % 4
    block = (y - at // 4) % 4 * 4 + (z_hi ^ (at % 4))
    right_table = (block - core) % 2 * 8 + (block // 2 - x) % 4 * 2 + (block // 8 - z_lo) % 2
    return left_table, right_table


def on_device(left_factor, right_factor, pair_grad, projection):
    shared, channels, rows = left_factor.shape
    held, entries, cols = right_factor.shape
    left_flat = jnp.transpose(left_factor, (0, 2, 1)).reshape(shared, rows * channels)
    right_flat = right_factor.reshape(held, entries * cols)
    weights = jnp.swapaxes(projection.reshape(channels, entries, -1), 0, 1).reshape(projection.shape)

    blocks = 4 * 4
    inverse = 1.0 / (blocks * shared)
    left_table, right_table = orders(blocks)
    left_table, right_table, weights = lax.optimization_barrier((left_table, right_table, weights))

    from_z = swapped(right_flat, "z_lo", 1)
    from_hi = swapped(left_flat, "z_hi", 1)
    pair_grad = pltpu.with_memory_space_constraint(pair_grad, pltpu.HBM)
    piece, token, pair_grad = expand(pair_grad, weights, channels, 0)
    expanded = [piece]
    near_right, near_left, token = join([[right_flat, from_z], [left_flat, from_hi]], [token])
    from_x = [moved(near_right, "x", d) for d in (1, 2, 3)]
    from_hi = swapped(near_left, "z_hi", 2)
    for number in (1, 2):
        piece, token = expand(pair_grad, weights, channels, number, [token])
        expanded.append(piece)
    along_x, along_z, token = join([[near_right, *from_x], [near_left, from_hi]], [token])
    right_sources = [along_x, swapped(along_x, "core", 1)]
    left_sources = [along_z] + [moved(along_z, "y", d) for d in (1, 2, 3)]
    expanded.append(expand(pair_grad, weights, channels, 3, [token])[0])

    token, own, *others = left_partial(left_table, right_sources, expanded, held, inverse)
    right_own, *right_others = right_partial(right_table, left_sources, expanded, shared, inverse, token)

    left_terms = [moved(other, "y", d + 1) for d, other in enumerate(others)]
    right_terms = [swapped(other, "core", 1) for other in right_others]
    token, right_near, *pieces = split_sum(right_own, right_terms, 2 * held, stacked=True)
    right_terms = [moved(piece, "x", d + 1) for d, piece in enumerate(pieces)]
    left_sum = own
    for term in left_terms:
        left_sum = left_sum + term.astype(jnp.float32)
    nearest, next_one, opposite, last = column_sum(left_sum, [], shared, token)
    from_next = moved(last, "z_hi", -1)
    passed = moved(opposite, "z_hi", 1)
    passed = moved((next_one + passed.astype(jnp.float32)).astype(jnp.bfloat16), "z_hi", 1)
    left_grad = nearest + from_next.astype(jnp.float32) + passed.astype(jnp.float32)
    left_grad = jnp.swapaxes(left_grad.reshape(shared, rows, channels), 1, 2)

    for term in right_terms:
        right_near = right_near + term.astype(jnp.float32)
    right_grad = right_near[:held] + swapped(right_near[held:].astype(jnp.bfloat16), "z_lo", 1).astype(jnp.float32)
    return (left_grad, right_grad.reshape(held, entries, cols))


def solution(mesh):
    names = ("z_lo", "x", "core", "y", "z_hi")
    torus = Mesh(mesh.devices.reshape(2, 4, 2, 4, 4), names)
    return jax.shard_map(
        on_device,
        mesh=torus,
        in_specs=(P(COL, None, ROW), P(ROW, None, COL), P(ROW, None, COL), P()),
        out_specs=(P(COL, None, ROW), P(ROW, None, COL)),
        check_vma=False,
    )
```

```python
import jax
import jax.numpy as jnp
from jax import lax
from jax.experimental import pallas as pl
from jax.experimental.pallas import tpu as pltpu
from jax.sharding import Mesh
from jax.sharding import PartitionSpec as P

ROW = ("z_lo", "x", "core")
COL = ("y", "z_hi")
VMEM = 12 << 20
PIECES = 4
PARTS = 1
WHOLE = pl.BlockSpec(memory_space=pltpu.VMEM)
TABLE = pl.BlockSpec(memory_space=pltpu.SMEM)


def params():
    return pltpu.CompilerParams(vmem_limit_bytes=VMEM)


def expand(pair_grad, weights, channels, numbers, after=()):
    rows, width, cols = pair_grad.shape
    wide = weights.shape[0]
    entries = wide // channels
    held = rows // PIECES
    step = 2
    chunk = 8
    first = 0 in numbers

    def body(weight_ref, grad_ref, *rest):
        rest = rest[len(after) :]
        out_refs = rest[: len(numbers)]
        token_ref, *rest = rest[len(numbers) :]
        copies = []
        if first:
            source_ref = grad_ref
            grad_ref, sems = rest
            for k in range(rows // chunk):
                part = pl.ds(k * chunk, chunk)
                copies.append(pltpu.make_async_copy(source_ref.at[part], grad_ref.at[part], sems.at[k]))
                copies[k].start()
        for out_ref, number in zip(out_refs, numbers):
            for t in range(held // 2):
                if first and t * 2 % chunk == 0:
                    copies[t * 2 // chunk].wait()
                i = number * held + t * 2
                pair = jnp.concatenate([grad_ref[i], grad_ref[i + 1]], axis=1)
                base = t * 2 * channels
                for entry in range(0, entries, step):
                    piece = weight_ref[entry * channels : (entry + step) * channels, :]
                    value = jnp.dot(piece, pair, preferred_element_type=jnp.float32).astype(jnp.bfloat16)
                    for k in range(step):
                        block = value[k * channels : (k + 1) * channels]
                        stacked = jnp.concatenate([block[:, :cols], block[:, cols:]], axis=0)
                        side = (entry + k) * cols
                        out_ref[base : base + 2 * channels, side : side + cols] = stacked
        for copy in copies[held // chunk :]:
            copy.wait()
        token_ref[...] = out_refs[-1][:16, :128]

    moved_shape = pltpu.VMEM(pair_grad.shape, pair_grad.dtype)
    return pl.pallas_call(
        body,
        in_specs=[WHOLE, pl.BlockSpec(memory_space=pltpu.HBM) if first else WHOLE] + [WHOLE] * len(after),
        out_specs=[WHOLE] * (len(numbers) + (2 if first else 1)),
        out_shape=[
            *[pltpu.VMEM((held * channels, entries * cols), jnp.bfloat16)] * len(numbers),
            jax.ShapeDtypeStruct((16, 128), jnp.bfloat16),
        ]
        + ([moved_shape] if first else []),
        scratch_shapes=[pltpu.SemaphoreType.DMA((rows // chunk,))] if first else [],
        compiler_params=params(),
        cost_estimate=pl.CostEstimate(flops=4 * len(numbers) * held * wide * width * cols, transcendentals=0, bytes_accessed=1 << 20),
        name="expand",
    )(weights, pair_grad, *after)


def join(groups, after):
    parts = [part for group in groups for part in group]

    def body(*refs):
        source_refs = refs[: len(parts)]
        out_refs = refs[len(parts) + len(after) : -1]
        at = 0
        for group, out_ref in zip(groups, out_refs):
            top = 0
            for part in group:
                out_ref[top : top + part.shape[0], :] = source_refs[at][...]
                top += part.shape[0]
                at += 1
        refs[-1][...] = refs[len(parts)][...]

    shapes = [(sum(part.shape[0] for part in group), group[0].shape[1]) for group in groups] + [after[0].shape]
    return pl.pallas_call(
        body,
        in_specs=[WHOLE] * (len(parts) + len(after)),
        out_specs=[WHOLE] * len(shapes),
        out_shape=[jax.ShapeDtypeStruct(shape, jnp.bfloat16) for shape in shapes],
        compiler_params=params(),
        cost_estimate=pl.CostEstimate(flops=0, transcendentals=0, bytes_accessed=1 << 20),
        name="join",
    )(*parts, *after)


def place(scratch, table_ref, sources, size):
    at = 0
    for source in sources:
        for top in range(0, source.shape[0], size):
            scratch[table_ref[at]] = source[top : top + size, :]
            at += 1


def left_partial(table, sources, expanded, size, inverse):
    count = table.shape[0]
    sequences = count * size
    depth = expanded[0].shape[1]
    total = sum(e.shape[0] for e in expanded)
    part = sequences // 4
    block = 512

    def body(table_ref, *refs):
        source_refs = refs[: len(sources)]
        expanded_refs = refs[len(sources) : len(sources) + len(expanded)]
        token_ref, own_ref, *other_refs = refs[len(sources) + len(expanded) : -2]
        placed, turned = refs[-2:]
        place(placed, table_ref, source_refs, size)
        turned[...] = placed[...].reshape(sequences, depth).T
        at = 0
        for expanded_ref in expanded_refs:
            for top in range(0, expanded_ref.shape[0], block):
                value = jnp.dot(
                    expanded_ref[top : top + block, :], turned[...], preferred_element_type=jnp.float32
                )
                value = value.T * inverse
                own_ref[:, at : at + block] = value[:part]
                for k, other_ref in enumerate(other_refs):
                    lower = (k + 1) * part
                    other_ref[:, at : at + block] = value[lower : lower + part].astype(jnp.bfloat16)
                at += block
        token_ref[...] = other_refs[0][:16, :128]

    other = jax.ShapeDtypeStruct((part, total), jnp.bfloat16)
    return pl.pallas_call(
        body,
        in_specs=[TABLE] + [WHOLE] * (len(sources) + len(expanded)),
        out_specs=[WHOLE] * 5,
        out_shape=[
            jax.ShapeDtypeStruct((16, 128), jnp.bfloat16),
            jax.ShapeDtypeStruct((part, total), jnp.float32),
            other,
            other,
            other,
        ],
        scratch_shapes=[pltpu.VMEM((count, size, depth), jnp.bfloat16), pltpu.VMEM((depth, sequences), jnp.bfloat16)],
        compiler_params=params(),
        cost_estimate=pl.CostEstimate(flops=4 * sequences * depth * total, transcendentals=0, bytes_accessed=1 << 20),
        name="left_partial",
    )(table, *sources, *expanded)


def right_partial(table, sources, expanded, size, inverse, after):
    count = table.shape[0]
    sequences = count * size
    depth = sum(e.shape[0] for e in expanded)
    total = expanded[0].shape[1]
    part = sequences // 2
    block = 512

    def body(table_ref, *refs):
        source_refs = refs[: len(sources)]
        expanded_refs = refs[len(sources) : len(sources) + len(expanded)]
        own_ref, *other_refs, blocked, placed = refs[len(sources) + len(expanded) + 1 :]
        place(blocked, table_ref, source_refs, size)
        placed[...] = blocked[...].reshape(sequences, depth)
        for side in range(0, total, block):
            value = 0.0
            at = 0
            for expanded_ref in expanded_refs:
                high = expanded_ref.shape[0]
                value = value + jnp.dot(
                    placed[:, at : at + high],
                    expanded_ref[:, side : side + block],
                    preferred_element_type=jnp.float32,
                )
                at += high
            value = value * inverse
            own_ref[:, side : side + block] = value[:part]
            for k, other_ref in enumerate(other_refs):
                lower = part + k * (part // PARTS)
                other_ref[:, side : side + block] = value[lower : lower + part // PARTS].astype(other_ref.dtype)

    half = jax.ShapeDtypeStruct((part, total), jnp.float32)
    other = jax.ShapeDtypeStruct((part // PARTS, total), jnp.float32)
    return pl.pallas_call(
        body,
        in_specs=[TABLE] + [WHOLE] * (len(sources) + len(expanded) + 1),
        out_specs=[WHOLE] * (1 + PARTS),
        out_shape=[half] + [other] * PARTS,
        scratch_shapes=[pltpu.VMEM((count, size, depth), jnp.bfloat16), pltpu.VMEM((sequences, depth), jnp.bfloat16)],
        compiler_params=params(),
        cost_estimate=pl.CostEstimate(flops=2 * sequences * depth * total, transcendentals=0, bytes_accessed=1 << 20),
        name="right_partial",
    )(table, *sources, *expanded, after)


def column_sum(own, others, part, after):
    width = own.shape[1]

    def body(own_ref, *refs):
        total = own_ref[...]
        for ref in refs[: len(others)]:
            total = total + ref[...].astype(jnp.float32)
        for k, out_ref in enumerate(refs[len(others) + 1 :]):
            out_ref[...] = total[k * part : (k + 1) * part].astype(out_ref.dtype)

    return pl.pallas_call(
        body,
        in_specs=[WHOLE] * (2 + len(others)),
        out_specs=[WHOLE] * 4,
        out_shape=[jax.ShapeDtypeStruct((part, width), jnp.float32)] * 2
        + [jax.ShapeDtypeStruct((part, width), jnp.bfloat16)] * 2,
        compiler_params=params(),
        cost_estimate=pl.CostEstimate(flops=0, transcendentals=0, bytes_accessed=0),
        name="column_sum",
    )(own, *others, after)


def split_sum(own, others, part, after=(), stacked=False):
    rows, width = own.shape
    count = rows // part

    def body(*refs):
        given = refs[: 1 + len(others)]
        token_ref, near_ref, *piece_refs = refs[1 + len(others) + len(after) :]
        total = given[0][...]
        terms = [ref[...].astype(jnp.float32) for ref in given[1:]]
        if stacked:
            terms = [jnp.concatenate(terms, axis=0)]
        for term in terms:
            total = total + term
        near_ref[...] = total[:part]
        for k, piece_ref in enumerate(piece_refs):
            piece_ref[...] = total[(k + 1) * part : (k + 2) * part].astype(jnp.bfloat16)
        token_ref[...] = total[:8, :128]

    return pl.pallas_call(
        body,
        in_specs=[WHOLE] * (1 + len(others) + len(after)),
        out_specs=[WHOLE] * (1 + count),
        out_shape=[jax.ShapeDtypeStruct((8, 128), jnp.float32), jax.ShapeDtypeStruct((part, width), jnp.float32)]
        + [jax.ShapeDtypeStruct((part, width), jnp.bfloat16)] * (count - 1),
        compiler_params=params(),
        cost_estimate=pl.CostEstimate(flops=0, transcendentals=0, bytes_accessed=0),
        name="split_sum",
    )(own, *others, *after)


def moved(value, axis, distance):
    size = lax.axis_size(axis)
    return lax.ppermute(value, axis, [(k, (k + distance) % size) for k in range(size)])


def swapped(value, axis, bit):
    return lax.ppermute(value, axis, [(k, k ^ bit) for k in range(lax.axis_size(axis))])


def orders(blocks):
    z_lo, x, core, y, z_hi = (lax.axis_index(name) for name in ROW + COL)
    at = lax.iota(jnp.int32, blocks)
    block = (z_lo ^ (at % 2)) * 8 + (x - at // 2) % 4 * 2 + (core ^ (at // 8))
    left_table = (block // 4 - y) % 4 * 4 + (block - z_hi) % 4
    block = (y - at // 4) % 4 * 4 + (z_hi ^ (at % 4))
    right_table = (block - core) % 2 * 8 + (block // 2 - x) % 4 * 2 + (block // 8 - z_lo) % 2
    return left_table, right_table


def on_device(left_factor, right_factor, pair_grad, projection):
    shared, channels, rows = left_factor.shape
    held, entries, cols = right_factor.shape
    left_flat = jnp.transpose(left_factor, (0, 2, 1)).reshape(shared, rows * channels)
    right_flat = right_factor.reshape(held, entries * cols)
    weights = jnp.swapaxes(projection.reshape(channels, entries, -1), 0, 1).reshape(projection.shape)

    blocks = 4 * 4
    inverse = 1.0 / (blocks * shared)
    left_table, right_table = orders(blocks)
    left_table, right_table, weights = lax.optimization_barrier((left_table, right_table, weights))

    from_z = swapped(right_flat, "z_lo", 1)
    from_hi = swapped(left_flat, "z_hi", 1)
    pair_grad = pltpu.with_memory_space_constraint(pair_grad, pltpu.HBM)
    piece, token, pair_grad = expand(pair_grad, weights, channels, [0])
    expanded = [piece]
    near_right, near_left, token = join([[right_flat, from_z], [left_flat, from_hi]], [token])
    from_x = [moved(near_right, "x", d) for d in (1, 2, 3)]
    from_hi = swapped(near_left, "z_hi", 2)
    *pieces, token = expand(pair_grad, weights, channels, range(1, PIECES), [token])
    expanded += pieces
    along_x, along_z, token = join([[near_right, *from_x], [near_left, from_hi]], [token])
    right_sources = [along_x, swapped(along_x, "core", 1)]
    left_sources = [along_z] + [moved(along_z, "y", d) for d in (1, 2, 3)]

    token, own, *others = left_partial(left_table, right_sources, expanded, held, inverse)
    right_own, *right_others = right_partial(right_table, left_sources, expanded, shared, inverse, token)

    left_terms = [moved(other, "y", d + 1) for d, other in enumerate(others)]
    right_terms = [swapped(other, "core", 1) for other in right_others]
    token, right_near, *pieces = split_sum(right_own, right_terms, 2 * held, stacked=True)
    right_terms = [moved(piece, "x", d + 1) for d, piece in enumerate(pieces)]
    left_sum = own
    for term in left_terms:
        left_sum = left_sum + term.astype(jnp.float32)
    nearest, next_one, opposite, last = column_sum(left_sum, [], shared, token)
    from_next = moved(last, "z_hi", -1)
    passed = moved(opposite, "z_hi", 1)
    passed = moved((next_one + passed.astype(jnp.float32)).astype(jnp.bfloat16), "z_hi", 1)
    left_grad = nearest + from_next.astype(jnp.float32) + passed.astype(jnp.float32)
    left_grad = jnp.swapaxes(left_grad.reshape(shared, rows, channels), 1, 2)

    for term in right_terms:
        right_near = right_near + term.astype(jnp.float32)
    right_grad = right_near[:held] + swapped(right_near[held:].astype(jnp.bfloat16), "z_lo", 1).astype(jnp.float32)
    return (left_grad, right_grad.reshape(held, entries, cols))


def solution(mesh):
    names = ("z_lo", "x", "core", "y", "z_hi")
    torus = Mesh(mesh.devices.reshape(2, 4, 2, 4, 4), names)
    return jax.shard_map(
        on_device,
        mesh=torus,
        in_specs=(P(COL, None, ROW), P(ROW, None, COL), P(ROW, None, COL), P()),
        out_specs=(P(COL, None, ROW), P(ROW, None, COL)),
        check_vma=False,
    )
```
